32 devices in a mesh: shard: 2 (over x), heads: 4 (over z), tensor: 4 (over y, core).
Axes of the slice: x: 2, y: 2, z: 4, core: 2. Of those that a mesh axis runs over, the one named last changes fastest.
Arguments:
- latents: bfloat16 [6, 1024, 1152], P('shard', 'heads'), may hold values from -6 to 6
- conditioning: bfloat16 [6, 1152], P('shard'), may hold values from -6 to 6
- cotangent: bfloat16 [6, 1024, 1152], P('shard', 'heads'), may hold values from -6 to 6
- qkv_weight: bfloat16 [3, 1152, 1152], P(None, ('shard', 'heads'), 'tensor'), may hold values from -0.1875 to 0.1875
- attn_bias: bfloat16 [2, 1152], P(None, 'tensor'), may hold values from -3 to 3
- proj_weight: bfloat16 [1152, 1152], P('tensor', ('shard', 'heads')), may hold values from -3 to 3
- proj_bias: bfloat16 [1152], replicated, may hold values from -3 to 3
- up_weight: bfloat16 [1152, 4608], P(('shard', 'heads'), 'tensor'), may hold values from -0.1875 to 0.1875
- up_bias: bfloat16 [4608], P('tensor'), may hold values from -3 to 3
- down_weight: bfloat16 [4608, 1152], P('tensor', ('shard', 'heads')), may hold values from -0.09375 to 0.09375
- down_bias: bfloat16 [1152], replicated, may hold values from -3 to 3
- ada_weight: bfloat16 [1152, 6912], P(('shard', 'heads'), 'tensor'), may hold values from -0.1875 to 0.1875
- ada_bias: bfloat16 [6912], P('tensor'), may hold values from -3 to 3
Outputs:
- block_out: bfloat16 [6, 1024, 1152], P('shard', 'heads')
- grad_latents: bfloat16 [6, 1024, 1152], P('shard', 'heads')
- grad_cond: float32 [6, 1152], P('shard')
- grad_qkv: float32 [3, 1152, 1152], P(None, ('shard', 'heads'), 'tensor')
- grad_attnbias: float32 [2, 1152], P(None, 'tensor')
- grad_proj: float32 [1152, 1152], P('tensor', ('shard', 'heads'))
- grad_projbias: float32 [1152], replicated
- grad_up: float32 [1152, 4608], P(('shard', 'heads'), 'tensor')
- grad_upbias: float32 [4608], P('tensor')
- grad_down: float32 [4608, 1152], P('tensor', ('shard', 'heads'))
- grad_downbias: float32 [1152], replicated
- grad_ada: float32 [1152, 6912], P(('shard', 'heads'), 'tensor')
- grad_adabias: float32 [6912], P('tensor')
The draws below stay inside these ranges and needn't reach their ends.
All inputs are finite; a program needn't handle non-finite values.
Results may differ from the reference program's by a relative error of at most 0.014.
The reference program's roundings to bfloat16 on the way count: a program that leaves them out, or rounds other values in their place, can miss the bound.
Values may be sent and summed in bfloat16 or wider, within the bound.
No kernel may reach another device: no remote copies, remote signals or barrier semaphores. Data moves between devices by JAX's collectives and lax.ppermute only.
A program may use at most 192 MiB of HBM per device.

```python
import jax
import jax.numpy as jnp
from jax import lax

D = 1152
HEADS = 16
HEAD_DIM = 72
FF = 4608
SEQ = 1024
LATENTS = 6


def steps_of(own_key, shape, split, low, largest):
    gain, own = 1.0, jax.random.fold_in(own_key, 6)
    for axis_at, parts in split:
        heights = jnp.exp(jax.random.uniform(jax.random.fold_in(own, axis_at), (parts,), jnp.float32, low / len(split), largest / len(split)))
        gain = gain * jnp.repeat(heights, shape[axis_at] // parts).reshape([-1 if axis == axis_at else 1 for axis in range(len(shape))])
    return gain


def normal_values(stream_key, extent, spread, limit, split=(), kind=jnp.bfloat16):
    result = jax.random.normal(stream_key, extent, jnp.float32) * spread
    if len(split) > 0:
        result = steps_of(stream_key, extent, split, -0.22, 0.18) * result
    return jnp.clip(result, min=-limit, max=limit).astype(kind)


def setup_inputs(seed: int = 0) -> dict:
    splits = jax.random.split(jax.random.key(seed), 14)
    return {
        "latents": normal_values(splits[0], (LATENTS, SEQ, D), 1.0, 6.0, ((0, 2), (1, 4))),
        "conditioning": normal_values(splits[1], (LATENTS, D), 1.0, 6.0, ((0, 2),)),
        "cotangent": normal_values(splits[2], (LATENTS, SEQ, D), 1.0, 6.0, ((0, 2), (1, 4))),
        "qkv_weight": normal_values(splits[3], (3, D, D), D ** -0.5, 0.1875, ((1, 8), (2, 4))),
        "attn_bias": normal_values(splits[4], (2, D), 0.5, 3.0, ((1, 4),)),
        "proj_weight": normal_values(splits[5], (D, D), (max(4 * D // SEQ, 1)) ** -0.5, 3.0, ((0, 4), (1, 8))),
        "proj_bias": normal_values(splits[6], (D,), 0.5, 3.0),
        "up_weight": normal_values(splits[7], (D, FF), D ** -0.5, 0.1875, ((0, 8), (1, 4))),
        "up_bias": normal_values(splits[8], (FF,), 0.5, 3.0, ((0, 4),)),
        "down_weight": normal_values(splits[9], (FF, D), FF ** -0.5, 0.09375, ((0, 4), (1, 8))),
        "down_bias": normal_values(splits[10], (D,), 0.5, 3.0),
        "ada_weight": normal_values(splits[11], (D, 6 * D), D ** -0.5, 0.1875, ((0, 8), (1, 4))),
        "ada_bias": normal_values(splits[12], (6 * D,), 0.5, 3.0, ((0, 4),)),
    }


@jax.custom_vjp
def low(v):
    return lax.optimization_barrier(v.astype(jnp.bfloat16)).astype(jnp.float32)

@jax.custom_vjp
def low_back(v):
    return v

def low_keep(v):
    return (low(v), None)

def low_pass(kept, grad):
    return (grad,)

def back_keep(v):
    return (v, None)

def back_low(kept, grad):
    return (low(grad),)
low.defvjp(low_keep, low_pass)
low_back.defvjp(back_keep, back_low)
epsilon = 1e-06
tanh_scale = 0.7978845608028654
highest = lax.Precision.HIGHEST

def matmul(left, right):
    return jnp.dot(left, right, precision=highest, preferred_element_type=jnp.float32)

def normalize(inputs):
    centered = inputs - lax.optimization_barrier(jnp.mean(inputs, axis=-1, keepdims=True))
    return centered * lax.rsqrt(lax.optimization_barrier(jnp.mean(centered * centered, axis=-1, keepdims=True)) + epsilon)

def gelu_tanh(inputs):
    inner = tanh_scale * (inputs + 0.044715 * inputs * inputs * inputs)
    return 0.5 * inputs * (1.0 + jnp.tanh(inner))

def attend(query_rows, key_rows, value_rows):
    query_split = query_rows.reshape(SEQ, HEADS, HEAD_DIM)
    key_split = key_rows.reshape(SEQ, HEADS, HEAD_DIM)
    value_split = value_rows.reshape(SEQ, HEADS, HEAD_DIM)
    scores = low_back(jnp.einsum('qhd,khd->hqk', query_split, key_split, precision=highest) * HEAD_DIM ** (-0.5))
    row_max = lax.optimization_barrier(jnp.max(scores, axis=-1, keepdims=True))
    weights = jnp.exp(scores - row_max)
    probs = weights / lax.optimization_barrier(jnp.sum(weights, axis=-1, keepdims=True))
    attended = jnp.einsum('hqk,khd->qhd', low(probs), value_split, precision=highest)
    return attended.reshape(SEQ, D)

def latent_layer(params, inputs, cond_vector):
    qkv_weight, attn_bias, proj_weight, proj_bias, up_weight, up_bias, down_weight, down_bias, ada_weight, ada_bias = params
    cond_act = low(jax.nn.silu(cond_vector))
    modulation = low_back(matmul(cond_act[None, :], ada_weight)[0] + ada_bias).reshape(6, D)
    shift_attn, scale_attn, gate_attn = (modulation[0], modulation[1], modulation[2])
    shift_mlp, scale_mlp, gate_mlp = (modulation[3], modulation[4], modulation[5])
    hidden_attn = low(normalize(inputs) * (1.0 + scale_attn) + shift_attn)
    queries = low_back(low(matmul(hidden_attn, qkv_weight[0]) + attn_bias[0]))
    keys_all = low_back(low(matmul(hidden_attn, qkv_weight[1])))
    values_all = low_back(low(matmul(hidden_attn, qkv_weight[2]) + attn_bias[1]))
    attended = low_back(low(attend(queries, keys_all, values_all)))
    branch_attn = low_back(matmul(attended, proj_weight) + proj_bias)
    middle = inputs + gate_attn * branch_attn
    hidden_mlp = low(normalize(middle) * (1.0 + scale_mlp) + shift_mlp)
    pre_act = low_back(matmul(hidden_mlp, up_weight) + up_bias)
    act_mlp = low(gelu_tanh(pre_act))
    branch_mlp = low_back(matmul(act_mlp, down_weight) + down_bias)
    return middle + gate_mlp * branch_mlp

def reference(latents, conditioning, cotangent, qkv_weight, attn_bias, proj_weight, proj_bias, up_weight, up_bias, down_weight, down_bias, ada_weight, ada_bias):
    params = tuple((source.astype(jnp.float32) for source in (qkv_weight, attn_bias, proj_weight, proj_bias, up_weight, up_bias, down_weight, down_bias, ada_weight, ada_bias)))

    def forward(weights_all, inputs, cond_all):

        def one_latent(paired):
            return latent_layer(weights_all, paired[0], paired[1])
        return lax.map(jax.checkpoint(one_latent), (inputs, cond_all))
    outputs, pullback = jax.vjp(forward, params, latents.astype(jnp.float32), conditioning.astype(jnp.float32))
    weight_grads, latents_grad, cond_grad = pullback(cotangent.astype(jnp.float32))
    return (outputs.astype(jnp.bfloat16), latents_grad.astype(jnp.bfloat16), cond_grad, weight_grads[0], weight_grads[1], weight_grads[2], weight_grads[3], weight_grads[4], weight_grads[5], weight_grads[6], weight_grads[7], weight_grads[8], weight_grads[9])
```

```python
import jax
import jax.numpy as jnp
from jax import lax
from jax.experimental import pallas as pl
from jax.experimental.pallas import tpu as pltpu
from jax.sharding import PartitionSpec as P

HEAD_DIM = 72
epsilon = 1e-06
tanh_scale = 0.7978845608028654
f32 = jnp.float32
bf16 = jnp.bfloat16


def gelu_tanh(inputs):
    inner = tanh_scale * (inputs + 0.044715 * inputs * inputs * inputs)
    return 0.5 * inputs * (1.0 + jnp.tanh(inner))


def normalize(inputs):
    centered = inputs - jnp.mean(inputs, axis=-1, keepdims=True)
    inverse = lax.rsqrt(jnp.mean(centered * centered, axis=-1, keepdims=True) + epsilon)
    return (centered * inverse, inverse)


def norm_back(grad_norm, normed, inverse):
    mean_grad = jnp.mean(grad_norm, axis=-1, keepdims=True)
    mean_cross = jnp.mean(grad_norm * normed, axis=-1, keepdims=True)
    return inverse * (grad_norm - mean_grad - normed * mean_cross)


def ring(value, axis, step):
    count = lax.axis_size(axis)
    return lax.ppermute(value, axis, [(at, (at + step) % count) for at in range(count)])


def flip(value, axis, bit):
    count = lax.axis_size(axis)
    return lax.ppermute(value, axis, [(at, at ^ bit) for at in range(count)])


def pick(stacked, at, axis=0):
    return lax.dynamic_index_in_dim(stacked, at, axis, keepdims=False)


def place(count, entries):
    first = entries[0][1]
    total = jnp.zeros((count,) + first.shape, first.dtype)
    for at, value in entries:
        total = lax.dynamic_update_index_in_dim(total, value, at, 0)
    return total


def pair_sum(value, axis):
    count = lax.axis_size(axis)
    bit = 1
    while bit < count:
        value = value + flip(value, axis, bit)
        bit *= 2
    return value


def pair_gather(value, axis):
    count, index = lax.axis_size(axis), lax.axis_index(axis)
    held = [(index, value)]
    bit = 1
    while bit < count:
        block = jnp.stack([entry for _, entry in held])
        other = flip(block, axis, bit)
        held = held + [(at ^ bit, other[k]) for k, (at, _) in enumerate(held)]
        bit *= 2
    return place(count, held)


def after(value, *others):
    return lax.optimization_barrier((value,) + others)[0]


def gather_rows(own, cross_after=None):
    rows, columns = own.shape
    z = lax.axis_index("heads")
    zn, xn = lax.axis_size("heads"), lax.axis_size("shard")
    parts = 2 if rows % 16 == 0 else 1
    own = own.reshape(parts, rows // parts, columns)
    left, right = ring(own, "heads", 1), ring(own, "heads", -1)
    far = [ring(left[:1], "heads", 1), ring(right[1:], "heads", -1)][:parts]
    if cross_after is not None:
        own = after(own, cross_after)
    pieces = [(z, 0, own), ((z + zn - 1) % zn, 0, left), ((z + 1) % zn, 0, right)]
    pieces += [((z + 2) % zn, part, piece) for part, piece in enumerate(far)]
    sides = 2 if xn == 2 else 1
    total = jnp.zeros((sides, zn) + own.shape, own.dtype)
    x = lax.axis_index("shard") if xn == 2 else 0
    for at, part, piece in pieces:
        total = lax.dynamic_update_slice(total, piece[None, None], (x, at, part, 0, 0))
        if xn == 2:
            other = flip(piece, "shard", 1)
            total = lax.dynamic_update_slice(total, other[None, None], (1 - x, at, part, 0, 0))
    total = total.reshape(sides * zn * rows, columns)
    total = total if xn == 2 else lax.all_gather(total, "shard", axis=0, tiled=True)
    return total, far


def scatter_rows(grad):
    z = lax.axis_index("heads")
    zn, xn = lax.axis_size("heads"), lax.axis_size("shard")
    rows = grad.shape[0] // (xn * zn)
    half = rows // 2 // 8 * 8
    if xn == 2:
        x = lax.axis_index("shard")

        def block(side, at):
            return lax.dynamic_slice_in_dim(grad, (side * zn + at) * rows, rows, 0)

        def summed(step):
            at = (z + step) % zn
            return block(x, at) + flip(block(1 - x, at).astype(bf16), "shard", 1).astype(f32)

        across, after, before, mine = summed(2), summed(1), summed(zn - 1), summed(0)
    else:
        parts = lax.psum_scatter(
            grad.reshape(xn, zn * rows, -1).astype(bf16), "shard", scatter_dimension=0
        ).reshape(zn, rows, -1)
        across, after, before, mine = (
            pick(parts, (z + step) % zn).astype(f32) for step in (2, 1, zn - 1, 0)
        )
    low = across.astype(bf16)
    from_left, from_right = ring(low[:half], "heads", 1), ring(low[half:], "heads", -1)
    after = jnp.concatenate([after[:half] + from_left.astype(f32), after[half:]]).astype(bf16)
    before = jnp.concatenate([before[:half], before[half:] + from_right.astype(f32)]).astype(bf16)
    return mine + (ring(after, "heads", 1).astype(f32) + ring(before, "heads", -1).astype(f32))


ORDER = (0, 2, 1, 3)


def to_relative(value):
    index = lax.axis_index("tensor")
    quarter = value.shape[1] // 4
    return jnp.concatenate(
        [lax.dynamic_slice_in_dim(value, (index ^ k) * quarter, quarter, 1) for k in ORDER], axis=1
    )


def own_quarter(value):
    return value[:, : value.shape[1] // 4]


def scatter_tokens(part):
    half, quarter = part.shape[1] // 2, part.shape[1] // 4
    sent = part[:, half:].astype(bf16)
    part = part[:, :half] + flip(sent, "tensor", 1).astype(f32)
    sent = part[:, quarter:].astype(bf16)
    return part[:, :quarter] + flip(sent, "tensor", 2).astype(f32)


def gather_tokens(own):
    pair = jnp.concatenate([own, flip(own, "tensor", 2)], axis=1)
    return jnp.concatenate([pair, flip(pair, "tensor", 1)], axis=1)


def gather_in_order(own):
    index = lax.axis_index("tensor")
    across = flip(own, "tensor", 2)
    beside, both = flip(own, "tensor", 1), flip(across, "tensor", 1)
    quarter = own.shape[1]
    total = jnp.zeros((own.shape[0], 4 * quarter, own.shape[2]), own.dtype)
    for piece, k in ((own, 0), (across, 2), (beside, 1), (both, 3)):
        total = lax.dynamic_update_slice_in_dim(total, piece, (index ^ k) * quarter, 1)
    return total


def exchange(value):
    return lax.all_to_all(value, "heads", split_axis=0, concat_axis=0, tiled=True)


def attend_kernel(qkv_ref, out_ref, wide_ref, probs_ref, scale_ref):
    blocks, _, _, tokens = qkv_ref.shape
    key = jnp.concatenate([qkv_ref[k, 1] for k in range(blocks)], axis=1)
    value = jnp.concatenate([qkv_ref[k, 2] for k in range(blocks)], axis=1)
    scaling = HEAD_DIM ** (-0.5)
    for k in range(blocks):
        scores = lax.dot_general(
            key, qkv_ref[k, 0], (((0,), (0,)), ((), ())), preferred_element_type=f32
        )
        scores = scores * scaling
        weights = jnp.exp(scores - jnp.max(scores, axis=0, keepdims=True))
        inverse = 1.0 / jnp.sum(weights, axis=0, keepdims=True)
        low = weights.astype(bf16)
        attended = jnp.dot(value, low, preferred_element_type=f32) * inverse
        out_ref[k] = attended.astype(bf16)
        wide_ref[k] = attended
        probs_ref[0, :, k * tokens : (k + 1) * tokens] = low
        scale_ref[0, :, k * tokens : (k + 1) * tokens] = inverse


def attend(qkv, count):
    blocks, _, width, total = qkv.shape
    tokens = total // count
    keys = blocks * tokens
    return pl.pallas_call(
        attend_kernel,
        grid=(count,),
        in_specs=[pl.BlockSpec((blocks, 3, width, tokens), lambda n: (0, 0, 0, n))],
        out_specs=[
            pl.BlockSpec((blocks, width, tokens), lambda n: (0, 0, n)),
            pl.BlockSpec((blocks, width, tokens), lambda n: (0, 0, n)),
            pl.BlockSpec((1, keys, keys), lambda n: (n, 0, 0)),
            pl.BlockSpec((1, 1, keys), lambda n: (n, 0, 0)),
        ],
        out_shape=[
            jax.ShapeDtypeStruct((blocks, width, total), bf16),
            jax.ShapeDtypeStruct((blocks, width, total), f32),
            jax.ShapeDtypeStruct((count, keys, keys), bf16),
            jax.ShapeDtypeStruct((count, 1, keys), f32),
        ],
        cost_estimate=pl.CostEstimate(
            flops=4 * count * keys * keys * width,
            bytes_accessed=count * keys * (2 * keys + 12 * width),
            transcendentals=count * keys * keys,
        ),
        name="attend",
    )(qkv)


def attend_back_kernel(qkv_ref, wide_ref, probs_ref, scale_ref, grad_ref, out_ref):
    blocks, _, _, tokens = qkv_ref.shape
    key = jnp.concatenate([qkv_ref[k, 1] for k in range(blocks)], axis=1)
    value = jnp.concatenate([qkv_ref[k, 2] for k in range(blocks)], axis=1)
    scaling = HEAD_DIM ** (-0.5)
    d_key = d_value = None
    for k in range(blocks):
        grad = grad_ref[k]
        wide_grad = grad.astype(f32)
        inverse = scale_ref[0, :, k * tokens : (k + 1) * tokens]
        low = probs_ref[0, :, k * tokens : (k + 1) * tokens]
        d_probs = lax.dot_general(
            value, grad, (((0,), (0,)), ((), ())), preferred_element_type=f32
        )
        mean = jnp.sum(wide_grad * wide_ref[k], axis=0, keepdims=True)
        d_scores = (low.astype(f32) * ((d_probs - mean) * inverse)).astype(bf16)
        d_query = jnp.dot(key, d_scores, preferred_element_type=f32)
        out_ref[k, 0] = (d_query * scaling).astype(bf16)
        add_key = lax.dot_general(
            qkv_ref[k, 0], d_scores, (((1,), (1,)), ((), ())), preferred_element_type=f32
        )
        add_value = lax.dot_general(
            (wide_grad * inverse).astype(bf16),
            low,
            (((1,), (1,)), ((), ())),
            preferred_element_type=f32,
        )
        d_key = add_key if k == 0 else d_key + add_key
        d_value = add_value if k == 0 else d_value + add_value
    for k in range(blocks):
        part = slice(k * tokens, (k + 1) * tokens)
        out_ref[k, 1] = (d_key[:, part] * scaling).astype(bf16)
        out_ref[k, 2] = d_value[:, part].astype(bf16)


def attend_back(qkv, wide, probs, scale, grad, count):
    blocks, _, width, total = qkv.shape
    tokens = total // count
    keys = blocks * tokens
    return pl.pallas_call(
        attend_back_kernel,
        grid=(count,),
        in_specs=[
            pl.BlockSpec((blocks, 3, width, tokens), lambda n: (0, 0, 0, n)),
            pl.BlockSpec((blocks, width, tokens), lambda n: (0, 0, n)),
            pl.BlockSpec((1, keys, keys), lambda n: (n, 0, 0)),
            pl.BlockSpec((1, 1, keys), lambda n: (n, 0, 0)),
            pl.BlockSpec((blocks, width, tokens), lambda n: (0, 0, n)),
        ],
        out_specs=pl.BlockSpec((blocks, 3, width, tokens), lambda n: (0, 0, 0, n)),
        out_shape=jax.ShapeDtypeStruct(qkv.shape, bf16),
        cost_estimate=pl.CostEstimate(
            flops=8 * count * keys * keys * width,
            bytes_accessed=count * keys * (2 * keys + 18 * width),
            transcendentals=0,
        ),
        name="attend_back",
    )(qkv, wide, probs, scale, grad)


def pack_kernel(qkv_ref, proj_ref, out_ref):
    heads = qkv_ref.shape[2] // HEAD_DIM
    columns = [
        qkv_ref[c, :, h * HEAD_DIM : (h + 1) * HEAD_DIM] for h in range(heads) for c in range(3)
    ]
    out_ref[...] = jnp.concatenate(columns + [proj_ref[...]], axis=1)


def pack(qkv_weight, proj):
    rows, columns = qkv_weight.shape[1], 3 * qkv_weight.shape[2] + proj.shape[1]
    return pl.pallas_call(
        pack_kernel, out_shape=jax.ShapeDtypeStruct((rows, columns), bf16), name="pack"
    )(qkv_weight, proj)


def unpack_kernel(value_ref, out_ref):
    heads = out_ref.shape[2] // HEAD_DIM
    for c in range(3):
        out_ref[c] = jnp.concatenate(
            [
                value_ref[:, (3 * h + c) * HEAD_DIM : (3 * h + c + 1) * HEAD_DIM]
                for h in range(heads)
            ],
            axis=1,
        )


def unpack(value):
    rows, columns = value.shape
    return pl.pallas_call(
        unpack_kernel, out_shape=jax.ShapeDtypeStruct((3, rows, columns // 3), f32), name="unpack"
    )(value)


def dot(spec, left, right):
    return jnp.einsum(spec, left, right, preferred_element_type=f32)


def shards(
    latents,
    conditioning,
    cotangent,
    qkv_weight,
    attn_bias,
    proj_weight,
    proj_bias,
    up_weight,
    up_bias,
    down_weight,
    down_bias,
    ada_weight,
    ada_bias,
):
    count, tokens, width = latents.shape
    local = attn_bias.shape[1]
    heads = local // HEAD_DIM
    rows = ada_weight.shape[0]
    xn, zn = lax.axis_size("shard"), lax.axis_size("heads")
    x, z, t = lax.axis_index("shard"), lax.axis_index("heads"), lax.axis_index("tensor")
    first = (x * zn + z) * rows

    cond_float = conditioning.astype(f32)
    cond_act = jax.nn.silu(cond_float).astype(bf16)
    cond_all = pair_gather(cond_act, "shard").reshape(xn * count, width)
    cond_rows = lax.dynamic_slice_in_dim(cond_all, first, rows, 1)
    mod_part = dot("ld,de->le", cond_rows, ada_weight).reshape(xn, count, -1)
    if xn == 2:
        mod_part = pick(mod_part, x) + flip(pick(mod_part, 1 - x), "shard", 1)
    else:
        mod_part = pick(pair_sum(mod_part, "shard"), x)
    packed, far = gather_rows(after(pack(qkv_weight, proj_weight.T), cond_all), mod_part)
    qkv_full, proj_full = packed[:, : 3 * local], packed[:, 3 * local :]
    up_full, far = gather_rows(after(up_weight, *far))
    down_full, _ = gather_rows(after(down_weight.T, *far))
    mod_part = pair_sum(mod_part, "heads") + ada_bias.astype(f32)
    modulation = pair_gather(mod_part, "tensor").transpose(1, 0, 2).reshape(count, 6, 1, width)

    bias_float = attn_bias.astype(f32)
    bias_float = bias_float.reshape(2, heads, HEAD_DIM)
    qkv_bias = jnp.stack([bias_float[0], jnp.zeros_like(bias_float[0]), bias_float[1]], axis=1)
    qkv_bias = qkv_bias.reshape(3 * local)

    latents_own = to_relative(latents)
    cotangent_own = to_relative(cotangent)
    flat = count * tokens
    shift_attn, scale_attn, gate_attn, shift_mlp, scale_mlp, gate_mlp = (
        modulation[:, k] for k in range(6)
    )
    norm_attn, _ = normalize(latents_own.astype(f32))
    hidden_attn = (norm_attn * (1.0 + scale_attn) + shift_attn).astype(bf16).reshape(flat, width)
    projected = (dot("de,rd->er", qkv_full, hidden_attn) + qkv_bias[:, None]).astype(bf16)
    split = exchange(projected.reshape(heads, 3, HEAD_DIM, flat))
    attended, wide, probs, sums = attend(split, count)
    attended = exchange(attended).reshape(local, flat)
    branch_attn = dot("er,de->rd", attended, proj_full).reshape(count, tokens, width)
    branch_attn = scatter_tokens(branch_attn) + proj_bias.astype(f32)
    inputs = own_quarter(latents_own).astype(f32)
    middle = inputs + gate_attn * branch_attn
    norm_mlp, inverse_mlp = normalize(middle)
    hidden_mlp = (norm_mlp * (1.0 + scale_mlp) + shift_mlp).astype(bf16)
    hidden_mlp = gather_tokens(hidden_mlp).reshape(flat, width)
    pre_act = dot("rd,df->rf", hidden_mlp, up_full) + up_bias.astype(f32)
    gelu_value, gelu_pull = jax.vjp(gelu_tanh, pre_act)
    act = gelu_value.astype(bf16)
    d_mlp = (gate_mlp * cotangent_own.astype(f32)).astype(bf16).reshape(flat, width)
    d_act = dot("rd,df->rf", d_mlp, down_full)
    d_pre = gelu_pull(d_act)[0].astype(bf16)
    d_hidden = dot("rf,df->rd", d_pre, up_full).reshape(count, tokens, width)
    d_hidden = scatter_tokens(d_hidden)
    grad_out = own_quarter(cotangent_own).astype(f32)
    grad_scale_mlp = jnp.sum(d_hidden * norm_mlp, axis=1)
    grad_shift_mlp = jnp.sum(d_hidden, axis=1)
    d_middle = grad_out + norm_back(d_hidden * (1.0 + scale_mlp), norm_mlp, inverse_mlp)
    grad_gate_attn = jnp.sum(d_middle * branch_attn, axis=1)
    d_attn = gather_tokens((gate_attn * d_middle).astype(bf16)).reshape(flat, width)
    d_attended = dot("rd,de->er", d_attn, proj_full).astype(bf16)
    d_attended = exchange(d_attended.reshape(heads, HEAD_DIM, flat))
    branch_mlp = dot("rf,df->rd", act, down_full).reshape(count, tokens, width)
    branch_mlp = scatter_tokens(branch_mlp) + down_bias.astype(f32)
    block_out = gather_in_order((middle + gate_mlp * branch_mlp).astype(bf16))
    grad_gate_mlp = jnp.sum(grad_out * branch_mlp, axis=1)
    down_grad = scatter_rows(dot("rd,rf->df", d_mlp, act)).T
    up_grad = scatter_rows(dot("rd,rf->df", hidden_mlp, d_pre))
    proj_grad = scatter_rows(dot("rd,er->de", d_attn, attended)).T
    d_qkv = exchange(attend_back(split, wide, probs, sums, d_attended, count))
    d_qkv = d_qkv.reshape(3 * local, flat)
    qkv_grad = unpack(scatter_rows(dot("rd,er->de", hidden_attn, d_qkv)))
    d_hidden = dot("er,de->rd", d_qkv, qkv_full).reshape(count, tokens, width)
    grad_scale_attn = jnp.sum(d_hidden * norm_attn, axis=1)
    grad_shift_attn = jnp.sum(d_hidden, axis=1)
    d_hidden = scatter_tokens(d_hidden)
    norm_attn, inverse_attn = normalize(inputs)
    d_inputs = d_middle + norm_back(d_hidden * (1.0 + scale_attn), norm_attn, inverse_attn)
    latents_grad = gather_in_order(d_inputs.astype(bf16))
    mod_grad = jnp.stack(
        (
            grad_shift_attn,
            grad_scale_attn,
            grad_gate_attn,
            grad_shift_mlp,
            grad_scale_mlp,
            grad_gate_mlp,
        ),
        axis=1,
    )

    def ones_sum(value):
        return jnp.sum(value.astype(f32), axis=0)

    columns = ada_bias.shape[0]
    mod_grad = mod_grad.reshape(count, 2, 2, columns)
    y, core = t // 2, t % 2
    mod_grad = pick(mod_grad, y, 1) + flip(pick(mod_grad, 1 - y, 1), "tensor", 2)
    mod_grad = pick(mod_grad, core, 1) + flip(pick(mod_grad, 1 - core, 1), "tensor", 1)
    small = jnp.concatenate(
        [
            mod_grad.reshape(count * columns),
            jnp.sum(d_qkv.astype(f32), axis=1),
            ones_sum(d_pre),
            ones_sum(d_mlp),
            ones_sum(d_attn),
        ]
    )
    small = pair_gather(pair_sum(small, "heads"), "shard")
    mod_all = small[:, : count * columns].astype(bf16).reshape(xn * count, columns)
    ada_grad = dot("ld,le->de", cond_rows, mod_all)
    ada_bias_grad = jnp.sum(mod_all.astype(f32), axis=0)
    biases = jnp.sum(small[:, count * columns :], axis=0)
    hidden = up_bias.shape[0]
    late = biases[: 3 * local].reshape(heads, 3, HEAD_DIM)
    attn_bias_grad = jnp.stack((late[:, 0], late[:, 2])).reshape(2, local)
    up_bias_grad = biases[3 * local : 3 * local + hidden]
    down_bias_grad = biases[3 * local + hidden : 3 * local + hidden + width]
    proj_bias_grad = biases[3 * local + hidden + width :]
    cond_part = pair_sum(dot("le,de->ld", mod_all, ada_weight), "tensor")
    cond_part = pair_gather(cond_part, "heads").reshape(zn, xn, count, rows)
    if xn == 2:
        mine = pick(cond_part, x, 1)
        other = flip(pick(cond_part, 1 - x, 1), "shard", 1)
        cond_part = place(2, [(x, mine), (1 - x, other)])
    else:
        cond_part = pick(pair_gather(cond_part, "shard"), x, 2)
    d_cond_act = cond_part.transpose(2, 0, 1, 3).reshape(count, width)
    _, silu_pull = jax.vjp(jax.nn.silu, cond_float)
    cond_grad = silu_pull(d_cond_act)[0]
    return (
        block_out,
        latents_grad,
        cond_grad,
        qkv_grad,
        attn_bias_grad,
        proj_grad,
        proj_bias_grad,
        up_grad,
        up_bias_grad,
        down_grad,
        down_bias_grad,
        ada_grad,
        ada_bias_grad,
    )


def solution(mesh):
    in_specs = (
        P("shard", "heads", None),
        P("shard", None),
        P("shard", "heads", None),
        P(None, ("shard", "heads"), "tensor"),
        P(None, "tensor"),
        P("tensor", ("shard", "heads")),
        P(),
        P(("shard", "heads"), "tensor"),
        P("tensor"),
        P("tensor", ("shard", "heads")),
        P(),
        P(("shard", "heads"), "tensor"),
        P("tensor"),
    )
    out_specs = (
        P("shard", "heads", None),
        P("shard", "heads", None),
        P("shard", None),
        P(None, ("shard", "heads"), "tensor"),
        P(None, "tensor"),
        P("tensor", ("shard", "heads")),
        P(),
        P(("shard", "heads"), "tensor"),
        P("tensor"),
        P("tensor", ("shard", "heads")),
        P(),
        P(("shard", "heads"), "tensor"),
        P("tensor"),
    )
    return jax.shard_map(shards, mesh=mesh, in_specs=in_specs, out_specs=out_specs, check_vma=False)
```
